256 devices in a mesh: view: 4 (over y_hi, core), tile: 64 (over z, y_lo, x).
Axes of the slice: x: 4, y: 4 (y_hi: 2, y_lo: 2; y = y_hi * 2 + y_lo), z: 8, core: 2. Of those that a mesh axis runs over, the one named last changes fastest.
Arguments:
- data: bfloat16 [8, 2560, 64, 128], P('view', 'tile'), may hold values from 0.1 to 5, as said below
- estimate: float32 [2560, 64, 128], P('tile'), may hold values from 0.5 to 2
- psf_taps: float32 [8, 3, 31], P('view'), may hold values from 0.03 to 1.6, as said below
Outputs:
- restored: float32 [2560, 64, 128], P('tile')
The draws below stay inside these ranges and needn't reach their ends.
Inputs may be any that keep to these rules, and one draw needn't show every extreme that they name: `data`: positive recorded intensities. `psf_taps`: positive taps.
All inputs are finite; a program needn't handle non-finite values.
Results may differ from the reference program's by a relative error of at most 0.0003.
Values may be sent and summed in bfloat16 or wider, within the bound.
A program may use at most 64 MiB of HBM per device.

```python
import math
import jax
import jax.numpy as jnp
from jax import lax

TAPS = 31
CX = 40
NY = 64
NZ = 128
ITERS = 3
VIEWS = 8
NX = 2560


def spread_blocks(coarse):
    wider = jnp.repeat(coarse, 4, axis=1)
    wider = jnp.repeat(wider, 4, axis=2)
    return jnp.repeat(wider, 8, axis=3)


def draw_data(key, part):
    key_common = jax.random.fold_in(key, 11)
    key_own = jax.random.fold_in(key, 12)
    key_bright = jax.random.fold_in(key, 13)
    key_dark = jax.random.fold_in(key, 14)
    coarse_shape = (NX // 4, NY // 4, NZ // 8)
    full_shape = (VIEWS, NX, NY, NZ)
    common = jax.random.uniform(key_common, (1,) + coarse_shape, dtype=jnp.float32)
    own = jax.random.uniform(key_own, (VIEWS,) + coarse_shape, dtype=jnp.float32)
    mixed = 0.6 * common + 0.4 * own
    bright_noise = jnp.clip(jax.random.normal(key_bright, full_shape, dtype=jnp.float32), -2.5, 2.5)
    dark_noise = jnp.clip(jax.random.normal(key_dark, full_shape, dtype=jnp.float32), -2.5, 2.5)
    bright = 4.0 * (1.0 + 0.1 * bright_noise)
    darker = 0.2 * (1.0 + 0.2 * dark_noise)
    level = 0.68
    inside = spread_blocks(mixed) > level
    return jnp.where(inside, bright, darker).astype(jnp.bfloat16)


def draw_psf_taps(key, part):
    key_width = jax.random.fold_in(key, 21)
    key_rough = jax.random.fold_in(key, 22)
    lower = jnp.array([1.5, 1.5, 3.0], dtype=jnp.float32)[None, :, None]
    upper = jnp.array([4.0, 4.0, 8.0], dtype=jnp.float32)[None, :, None]
    pick = jax.random.uniform(key_width, (VIEWS, 3, 1), dtype=jnp.float32)
    widths = lower * jnp.exp(pick * jnp.log(upper / lower))
    offsets = (jnp.arange(TAPS) - TAPS // 2).astype(jnp.float32)[None, None, :]
    envelope = jnp.exp(-0.5 * (offsets / widths) ** 2)
    rough = jax.random.uniform(key_rough, (VIEWS, 3, TAPS), dtype=jnp.float32, minval=0.6, maxval=1.4)
    return ((envelope + 0.06) * rough).astype(jnp.float32)


def block_levels(own_key, shape, shards, least, top_value):
    gain = 1.0
    for axis_at, blocks in shards:
        steps = jax.random.uniform(jax.random.fold_in(jax.random.fold_in(own_key, 6), axis_at), (blocks,), jnp.float32, least / len(shards), top_value / len(shards))
        gain = gain * jnp.repeat(jnp.exp(steps), shape[axis_at] // blocks).reshape((-1,) + (1,) * (len(shape) - 1 - axis_at))
    return gain


def setup_inputs(seed: int = 0) -> dict:
    key_of = jax.random.split(jax.random.key(seed), 4)
    data = draw_data(jax.random.fold_in(key_of[3], 71), 0)
    estimate = jnp.clip(jnp.exp(math.log(2.0) - 1.3862944 * jax.random.uniform(key_of[1], (NX, NY, NZ), jnp.float32) ** block_levels(key_of[1], (NX, NY, NZ), ((0, 64),), -0.2, 0.2)), 0.5, 2.0)
    psf_taps = draw_psf_taps(jax.random.fold_in(key_of[3], 71), 0)
    return dict(data=data, estimate=estimate, psf_taps=psf_taps)


highest = lax.Precision.HIGHEST


def band_matrix(coeffs, n_out, n_in, shift):
    row_index = jnp.arange(n_out)[:, None]
    col_index = jnp.arange(n_in)[None, :]
    offset = col_index - row_index + shift
    matches = offset[:, :, None] == jnp.arange(coeffs.shape[0])[None, None, :]
    return jnp.sum(jnp.where(matches, coeffs[None, None, :], 0.0 * coeffs[None, None, :]), axis=2)


def convolve_whole(field, kernel):
    half_width = kernel.shape[1] // 2
    padded = jnp.pad(field, ((half_width, CX - half_width), (0, 0), (0, 0)))
    blocks = padded.reshape(NX // CX + 1, CX, NY, NZ)
    along_x = band_matrix(kernel[0], CX, CX + 2 * half_width, 0)
    result = jnp.einsum("ij,bjyz->biyz", along_x[:, :CX], blocks[:-1], precision=highest)
    result = result + jnp.einsum("ij,bjyz->biyz", along_x[:, CX:], blocks[1:, :2 * half_width], precision=highest)
    result = result.reshape(NX, NY, NZ)
    along_y = band_matrix(kernel[1], NY, NY, half_width)
    along_z = band_matrix(kernel[2], NZ, NZ, half_width)
    result = jnp.einsum("yk,ikz->iyz", along_y, result, precision=highest)
    return jnp.einsum("iyk,zk->iyz", result, along_z, precision=highest)


def reference(data, estimate, psf_taps):
    flipped = psf_taps[:, :, ::-1]
    for step in range(ITERS):
        summed = jnp.zeros_like(estimate)
        for view_index in range(VIEWS):
            blurred = convolve_whole(estimate, psf_taps[view_index])
            ratios_here = data[view_index].astype(jnp.float32) / blurred
            summed = summed + convolve_whole(ratios_here, flipped[view_index])
        estimate = estimate * summed / VIEWS
    return estimate
```

```python
import jax
import jax.numpy as jnp
from jax import lax
from jax.experimental import pallas as pl
from jax.experimental.pallas import tpu as pltpu
from jax.sharding import PartitionSpec as P

ITERS = 3
GROUP = 4
F32 = jnp.float32
BF16 = jnp.bfloat16
MESH = pl.DeviceIdType.MESH


def band(taps, n_rows, n_cols, shift):
    offset = jnp.arange(n_cols)[None, :] - jnp.arange(n_rows)[:, None] + shift
    hit = offset[:, :, None] == jnp.arange(taps.shape[-1])[None, None, :]
    return jnp.sum(jnp.where(hit[None], taps[:, None, None, :], 0.0), axis=3)


def split(w):
    hi = w.astype(BF16)
    return hi, (w - hi.astype(F32)).astype(BF16)


def split_weights(w):
    hi = lax.reduce_precision(w, 8, 7)
    return hi.astype(BF16), (w - hi).astype(BF16)


def dot(a, b):
    return jnp.dot(a, b, preferred_element_type=F32)


def make_weights(taps, ny, nz, rows, ext, mid, ext_pad, mid_pad):
    half = taps.shape[2] // 2
    flipped = taps[:, :, ::-1]
    cat = jnp.concatenate

    def along_x(t, n_out, n_in, out_pad, in_pad):
        w = band(t, n_out, n_in, 0)
        w = jnp.pad(w, ((0, 0), (0, out_pad - n_out), (0, in_pad - n_in)))
        return cat(split_weights(w), axis=2)

    xf = along_x(taps[:, 0], mid, ext, mid_pad, ext_pad)
    xa = along_x(flipped[:, 0], rows, mid, rows, mid_pad)
    yf = cat(split_weights(band(taps[:, 1], ny, ny, half)), axis=2)
    hi, lo = split_weights(band(flipped[:, 1], ny, ny, half))
    ya = cat([hi, lo, hi], axis=2)
    hi, lo = split_weights(band(flipped[:, 2], nz, nz, half))
    zf = cat([cat([hi[0], hi[1]], axis=1), cat([lo[0], lo[1]], axis=1)], axis=0)
    hi, lo = split_weights(band(taps[:, 2], nz, nz, half))
    za = cat([cat([hi[0], lo[0]], axis=1), cat([hi[1], lo[1]], axis=1)], axis=0)
    return xf, yf, zf, xa, ya, za


def shards(data, estimate, psf_taps):
    views, rows, ny, nz = data.shape
    half = psf_taps.shape[2] // 2
    total_views = views * lax.axis_size("view")
    tiles = lax.axis_size("tile")
    wide = 2 * half
    ext = rows + 2 * wide
    mid = rows + 2 * half
    ext_pad = -(-ext // 16) * 16
    mid_pad = -(-mid // 16) * 16
    ch = rows // 4
    weights = make_weights(psf_taps, ny, nz, rows, ext, mid, ext_pad, mid_pad)

    def kernel(data_ref, est_ref, xf, yf, zf, xa, ya, za, out_ref,
               extb, zb, xb, rb, ab, yb, dx, em, ps, pr, po, hs, hr, fin,
               lsem, dsem_s, dsem_r, hsem_s, hsem_r, fsem_s, fsem_r,
               psem_s, psem_r, ysem_s, ysem_r, osem_s, osem_r):
        t = lax.axis_index("tile")
        v = lax.axis_index("view")
        c = lax.rem(v, 2)
        other = (v - c) + (1 - c)
        across = lax.rem(v + 2, 4)
        left = lax.rem(t + tiles - 1, tiles)
        right = lax.rem(t + 1, tiles)
        has_left = t > 0
        has_right = t < tiles - 1

        cp_est = pltpu.make_async_copy(est_ref, em, lsem.at[0])
        cp_dat = pltpu.make_async_copy(data_ref, dx.at[:, pl.ds(half, rows)], lsem.at[1])
        cp_est.start()
        cp_dat.start()

        barrier = pltpu.get_barrier_semaphore()
        for who in ((t, other), (t, across), (left, v), (right, v)):
            pl.semaphore_signal(barrier, inc=1, device_id=(who[1], who[0]), device_id_type=MESH)
        pl.semaphore_wait(barrier, 4)

        def remote(src, dst, s_sem, r_sem, tile, view):
            return pltpu.make_async_remote_copy(
                src_ref=src, dst_ref=dst, send_sem=s_sem, recv_sem=r_sem,
                device_id=(view, tile), device_id_type=MESH)

        inner = ch + ch * c
        outer = 3 * ch * c
        c_tile = jnp.where(c == 0, left, right)
        c_send = ((c == 0) & has_left) | ((c == 1) & has_right)
        c_recv = ((c == 0) & has_right) | ((c == 1) & has_left)

        def own(k, row):
            return extb.at[k, pl.ds(wide + row, ch)]

        def piece(k, which):
            if which == 0:
                src, at, tile, give, take = inner, ext - wide + ch + ch * c, left, has_left, has_right
            elif which == 1:
                src, at, tile, give, take = inner, ch * c, right, has_right, has_left
            else:
                src, at, tile, give, take = outer, (ext - wide) - (ext - wide - 2 * ch) * c, c_tile, c_send, c_recv
            return src, at, tile, give, take

        def halo(k, which):
            src, at, tile, give, take = piece(k, which)
            return remote(own(k, src), extb.at[k, pl.ds(at, ch)],
                          hsem_s.at[k, which], hsem_r.at[k, which], tile, v)

        def forward(k, which):
            src, at, tile, give, take = piece(k, which)
            return remote(extb.at[k, pl.ds(at, ch)], extb.at[k, pl.ds(at, ch)],
                          fsem_s.at[k, which], fsem_r.at[k, which], t, other)

        def forwarded(k, which):
            d = 1 - c
            if which == 0:
                at, take = ext - wide + ch + ch * d, has_right
            elif which == 1:
                at, take = ch * d, has_left
            else:
                at = (ext - wide) - (ext - wide - 2 * ch) * d
                take = ((d == 0) & has_right) | ((d == 1) & has_left)
            return remote(extb.at[k, pl.ds(at, ch)], extb.at[k, pl.ds(at, ch)],
                          fsem_s.at[k, which], fsem_r.at[k, which], t, other), take

        def start_halo(k, which):
            give = piece(k, which)[3]

            @pl.when(give)
            def _():
                halo(k, which).start()

        def finish_halo(k):
            for which in (0, 1, 2):
                take = piece(k, which)[4]

                @pl.when(take)
                def _():
                    halo(k, which).wait_recv()
                    forward(k, which).start()
            for which in (0, 1, 2):
                cp, take = forwarded(k, which)

                @pl.when(take)
                def _():
                    cp.wait_recv()

        def drain_halo(k):
            for which in (0, 1, 2):
                src, at, tile, give, take = piece(k, which)

                @pl.when(give)
                def _():
                    halo(k, which).wait_send()

                @pl.when(take)
                def _():
                    forward(k, which).wait_send()

        to_right = remote(data_ref.at[:, pl.ds(rows - half, half)], dx.at[:, pl.ds(0, half)],
                          dsem_s.at[0], dsem_r.at[0], right, v)
        to_left = remote(data_ref.at[:, pl.ds(0, half)], dx.at[:, pl.ds(half + rows, half)],
                         dsem_s.at[1], dsem_r.at[1], left, v)

        cp_est.wait()
        extb[0, pl.ds(wide, rows)] = em[...].astype(BF16)
        for which in (0, 1, 2):
            start_halo(0, which)

        @pl.when(has_right)
        def _():
            to_right.start()

        @pl.when(has_left)
        def _():
            to_left.start()

        @pl.when(t == 0)
        def _():
            for k in range(ITERS):
                extb[k, pl.ds(0, wide)] = jnp.zeros((wide, ny, nz), BF16)
            for i in range(views):
                dx[i, pl.ds(0, half)] = jnp.zeros((half, ny, nz), BF16)

        @pl.when(t == tiles - 1)
        def _():
            for k in range(ITERS):
                extb[k, pl.ds(ext - wide, wide)] = jnp.zeros((wide, ny, nz), BF16)
            for i in range(views):
                dx[i, pl.ds(half + rows, half)] = jnp.zeros((half, ny, nz), BF16)

        for i in range(views):
            zb[i, pl.ds(ext * ny, (ext_pad - ext) * ny), :] = jnp.zeros(((ext_pad - ext) * ny, nz), F32)
            rb[i, pl.ds(mid * ny, (mid_pad - mid) * ny), :] = jnp.zeros(((mid_pad - mid) * ny, nz), F32)

        def blur_z(k):
            step = ext // 10

            def body(j, _):
                lhs = extb[k, pl.ds(j * step, step)].reshape(step * ny, nz)
                o = dot(jnp.concatenate([lhs, lhs], axis=1), zf[...])
                at = pl.multiple_of(j * step * ny, step * ny)
                for i in range(views):
                    zb[i, pl.ds(at, step * ny), :] = o[:, i * nz:(i + 1) * nz]
                return 0
            lax.fori_loop(0, 10, body, 0)

        def conv_x(src, dst, w, n_in, n_out):
            def body(j, _):
                outs = []
                for u in range(GROUP):
                    y = 2 * (GROUP * j + u)
                    for i in range(views):
                        a = src[i, pl.ds(y, n_in, stride=ny), :]
                        b = src[i, pl.ds(y + 1, n_in, stride=ny), :]
                        r = jnp.concatenate([a, b], axis=1).astype(BF16)
                        outs.append((y, i, dot(w[i], jnp.concatenate([r, r], axis=0))))
                for y, i, o in outs:
                    dst[i, pl.ds(y, n_out, stride=ny), :] = o[:, :nz]
                    dst[i, pl.ds(y + 1, n_out, stride=ny), :] = o[:, nz:]
                return 0
            lax.fori_loop(0, ny // (2 * GROUP), body, 0)

        def ratios():
            def body(j, _):
                outs = []
                for u in range(5):
                    at = pl.multiple_of((5 * j + u) * 2 * ny, 2 * ny)
                    for i in range(views):
                        r = jnp.concatenate([xb[i, pl.ds(at, ny), :], xb[i, pl.ds(at + ny, ny), :]], axis=1).astype(BF16)
                        o = dot(yf[i], jnp.concatenate([r, r], axis=0))
                        row = 2 * (5 * j + u)
                        outs.append((at, i, dx[i, row].astype(F32) / o[:, :nz],
                                     dx[i, row + 1].astype(F32) / o[:, nz:]))
                for at, i, p, q in outs:
                    rb[i, pl.ds(at, ny), :] = p
                    rb[i, pl.ds(at + ny, ny), :] = q
                return 0
            lax.fori_loop(0, mid // 10, body, 0)

        def adjoint_rows(row):
            for j in range(ch // 2):
                at = pl.multiple_of((row + 2 * j) * ny, 2 * ny)
                to = j * 2 * ny
                for i in range(views):
                    r = jnp.concatenate([ab[i, pl.ds(at, ny), :], ab[i, pl.ds(at + ny, ny), :]], axis=1)
                    hi, lo = split(r)
                    o = dot(ya[i], jnp.concatenate([hi, hi, lo], axis=0))
                    yb[pl.ds(to, ny), i * nz:(i + 1) * nz] = o[:, :nz]
                    yb[pl.ds(to + ny, ny), i * nz:(i + 1) * nz] = o[:, nz:]
            hi, lo = split(yb[...])
            o = dot(hi, za[...])
            o = o[:, :nz] + o[:, nz:] + dot(lo, za[:, :nz])
            return o.reshape(ch, ny, nz)

        def partner(k, p):
            return remote(ps.at[k, p], pr.at[k, p], psem_s.at[k, p], psem_r.at[k, p], t, other)

        def over(k, p):
            return remote(hs.at[k, p], hr.at[k, p], ysem_s.at[k, p], ysem_r.at[k, p], t, across)

        def share(k, p):
            row = (inner, outer)[p]
            return remote(own(k + 1, row), own(k + 1, row), osem_s.at[k, p], osem_r.at[k, p], t, other)

        def shared(k, p):
            row = (ch + ch * (1 - c), 3 * ch * (1 - c))[p]
            return remote(own(k + 1, row), own(k + 1, row), osem_s.at[k, p], osem_r.at[k, p], t, other)

        finish_halo(0)
        cp_dat.wait()

        def iteration(k, _):
            blur_z(k)
            conv_x(zb, xb, xf, ext_pad, mid_pad)

            @pl.when((k == 0) & has_left)
            def _():
                to_right.wait_recv()

            @pl.when((k == 0) & has_right)
            def _():
                to_left.wait_recv()

            ratios()
            conv_x(rb, ab, xa, mid_pad, rows)
            theirs = (ch + ch * (1 - c), 3 * ch * (1 - c))
            ours = (inner, outer)
            for p in (0, 1):
                ps[k, p] = adjoint_rows(theirs[p])
                partner(k, p).start()
                po[p] = adjoint_rows(ours[p])
                partner(k, p).wait_recv()
                hs[k, p] = po[p] + pr[k, p]
                over(k, p).start()
            for p in (0, 1):
                over(k, p).wait_recv()
                rows_here = pl.ds(ours[p], ch)
                em[rows_here] = em[rows_here] * (hs[k, p] + hr[k, p]) / total_views

                @pl.when(k < ITERS - 1)
                def _():
                    extb[k + 1, pl.ds(wide + ours[p], ch)] = em[rows_here].astype(BF16)
                    for which in ((0, 1), (2,))[p]:
                        start_halo(k + 1, which)
                    share(k, p).start()

            @pl.when(k < ITERS - 1)
            def _():
                finish_halo(k + 1)
                for p in (0, 1):
                    shared(k, p).wait_recv()
            return 0

        lax.fori_loop(0, ITERS, iteration, 0)

        ends = []
        for p in (0, 1):
            row = (inner, outer)[p]
            fin[p] = em[pl.ds(row, ch)]
            here = pltpu.make_async_copy(fin.at[p], out_ref.at[pl.ds(row, ch)], lsem.at[2 + p])
            there = remote(fin.at[p], out_ref.at[pl.ds(row, ch)],
                           osem_s.at[ITERS - 1, p], osem_r.at[ITERS - 1, p], t, other)
            here.start()
            there.start()
            ends += [here, there]
        for cp in ends:
            cp.wait()

        @pl.when(has_right)
        def _():
            to_right.wait_send()

        @pl.when(has_left)
        def _():
            to_left.wait_send()

        for k in range(ITERS):
            drain_halo(k)
            for p in (0, 1):
                partner(k, p).wait_send()
                over(k, p).wait_send()
                if k < ITERS - 1:
                    share(k, p).wait_send()

    vmem = pltpu.VMEM
    dma = pltpu.SemaphoreType.DMA
    block = (ch, ny, nz)
    return pl.pallas_call(
        kernel,
        out_shape=jax.ShapeDtypeStruct(estimate.shape, F32),
        in_specs=[pl.BlockSpec(memory_space=pl.ANY)] * 2 + [pl.BlockSpec(memory_space=vmem)] * 6,
        out_specs=pl.BlockSpec(memory_space=pl.ANY),
        scratch_shapes=[
            vmem((ITERS, ext, ny, nz), BF16),
            vmem((views, ext_pad * ny, nz), F32),
            vmem((views, mid_pad * ny, nz), F32),
            vmem((views, mid_pad * ny, nz), F32),
            vmem((views, rows * ny, nz), F32),
            vmem((ch * ny, views * nz), F32),
            vmem((views, mid, ny, nz), BF16),
            vmem((rows, ny, nz), F32),
            vmem((ITERS, 2) + block, F32),
            vmem((ITERS, 2) + block, F32),
            vmem((2,) + block, F32),
            vmem((ITERS, 2) + block, F32),
            vmem((ITERS, 2) + block, F32),
            vmem((2,) + block, F32),
            dma((4,)), dma((2,)), dma((2,)),
            dma((ITERS, 3)), dma((ITERS, 3)), dma((ITERS, 3)), dma((ITERS, 3)),
            dma((ITERS, 2)), dma((ITERS, 2)), dma((ITERS, 2)), dma((ITERS, 2)),
            dma((ITERS, 2)), dma((ITERS, 2)),
        ],
        compiler_params=pltpu.CompilerParams(
            collective_id=0, has_side_effects=True, vmem_limit_bytes=60 * 1024 * 1024),
    )(data, estimate, *weights)


def solution(mesh):
    placed = (P("view", "tile", None, None), P("tile", None, None), P("view", None, None))
    return jax.shard_map(
        shards, mesh=mesh, in_specs=placed, out_specs=P("tile", None, None), check_vma=False
    )
```

```python
import jax
import jax.numpy as jnp
from jax import lax
from jax.experimental import pallas as pl
from jax.experimental.pallas import tpu as pltpu
from jax.sharding import PartitionSpec as P

ITERS = 3
GROUP = 4
ST = 65
F32 = jnp.float32
BF16 = jnp.bfloat16
MESH = pl.DeviceIdType.MESH


def band(taps, n_rows, n_cols, shift):
    offset = jnp.arange(n_cols)[None, :] - jnp.arange(n_rows)[:, None] + shift
    hit = offset[:, :, None] == jnp.arange(taps.shape[-1])[None, None, :]
    return jnp.sum(jnp.where(hit[None], taps[:, None, None, :], 0.0), axis=3)


def split(w):
    hi = w.astype(BF16)
    return hi, (w - hi.astype(F32)).astype(BF16)


def split_weights(w):
    hi = lax.reduce_precision(w, 8, 7)
    return hi.astype(BF16), (w - hi).astype(BF16)


def dot(a, b):
    return jnp.dot(a, b, preferred_element_type=F32)


def make_weights(taps, ny, nz, rows, ext, mid, ext_pad, mid_pad):
    half = taps.shape[2] // 2
    flipped = taps[:, :, ::-1]
    cat = jnp.concatenate

    def along_x(t, n_out, n_in, out_pad, in_pad):
        w = band(t, n_out, n_in, 0)
        w = jnp.pad(w, ((0, 0), (0, out_pad - n_out), (0, in_pad - n_in)))
        return cat(split_weights(w), axis=2)

    xf = along_x(taps[:, 0], mid, ext, mid_pad, ext_pad)
    xa = along_x(flipped[:, 0], rows, mid, rows, mid_pad)
    yf = cat(split_weights(band(taps[:, 1], ny, ny, half)), axis=2)
    hi, lo = split_weights(band(flipped[:, 1], ny, ny, half))
    ya = cat([hi, lo, hi], axis=2)
    hi, lo = split_weights(band(flipped[:, 2], nz, nz, half))
    zf = cat([cat([hi[0], hi[1]], axis=1), cat([lo[0], lo[1]], axis=1)], axis=0)
    hi, lo = split_weights(band(taps[:, 2], nz, nz, half))
    za = cat([cat([hi[0], lo[0]], axis=1), cat([hi[1], lo[1]], axis=1)], axis=0)
    return xf, yf, zf, xa, ya, za


def shards(data, estimate, psf_taps):
    views, rows, ny, nz = data.shape
    half = psf_taps.shape[2] // 2
    total_views = views * lax.axis_size("view")
    tiles = lax.axis_size("tile")
    wide = 2 * half
    ext = rows + 2 * wide
    mid = rows + 2 * half
    ext_pad = -(-ext // 16) * 16
    mid_pad = -(-mid // 16) * 16
    ch = rows // 4
    weights = make_weights(psf_taps, ny, nz, rows, ext, mid, ext_pad, mid_pad)

    def kernel(data_ref, est_ref, xf, yf, zf, xa, ya, za, out_ref,
               extb, zb, xb, rb, ab, yb, dx, em, ps, pr, po, hs, hr, fin,
               lsem, dsem_s, dsem_r, hsem_s, hsem_r, fsem_s, fsem_r,
               psem_s, psem_r, ysem_s, ysem_r, osem_s, osem_r):
        t = lax.axis_index("tile")
        v = lax.axis_index("view")
        c = lax.rem(v, 2)
        other = (v - c) + (1 - c)
        across = lax.rem(v + 2, 4)
        left = lax.rem(t + tiles - 1, tiles)
        right = lax.rem(t + 1, tiles)
        has_left = t > 0
        has_right = t < tiles - 1

        cp_est = pltpu.make_async_copy(est_ref, em, lsem.at[0])
        cp_dat = pltpu.make_async_copy(data_ref, dx.at[:, pl.ds(half, rows)], lsem.at[1])
        cp_est.start()
        cp_dat.start()

        barrier = pltpu.get_barrier_semaphore()
        for who in ((t, other), (t, across), (left, v), (right, v)):
            pl.semaphore_signal(barrier, inc=1, device_id=(who[1], who[0]), device_id_type=MESH)
        pl.semaphore_wait(barrier, 4)

        def remote(src, dst, s_sem, r_sem, tile, view):
            return pltpu.make_async_remote_copy(
                src_ref=src, dst_ref=dst, send_sem=s_sem, recv_sem=r_sem,
                device_id=(view, tile), device_id_type=MESH)

        inner = ch + ch * c
        outer = 3 * ch * c
        c_tile = jnp.where(c == 0, left, right)
        c_send = ((c == 0) & has_left) | ((c == 1) & has_right)
        c_recv = ((c == 0) & has_right) | ((c == 1) & has_left)

        def own(k, row):
            return extb.at[k, pl.ds(wide + row, ch)]

        def piece(k, which):
            if which == 0:
                src, at, tile, give, take = inner, ext - wide + ch + ch * c, left, has_left, has_right
            elif which == 1:
                src, at, tile, give, take = inner, ch * c, right, has_right, has_left
            else:
                src, at, tile, give, take = outer, (ext - wide) - (ext - wide - 2 * ch) * c, c_tile, c_send, c_recv
            return src, at, tile, give, take

        def halo(k, which):
            src, at, tile, give, take = piece(k, which)
            return remote(own(k, src), extb.at[k, pl.ds(at, ch)],
                          hsem_s.at[k, which], hsem_r.at[k, which], tile, v)

        def forward(k, which):
            src, at, tile, give, take = piece(k, which)
            return remote(extb.at[k, pl.ds(at, ch)], extb.at[k, pl.ds(at, ch)],
                          fsem_s.at[k, which], fsem_r.at[k, which], t, other)

        def forwarded(k, which):
            d = 1 - c
            if which == 0:
                at, take = ext - wide + ch + ch * d, has_right
            elif which == 1:
                at, take = ch * d, has_left
            else:
                at = (ext - wide) - (ext - wide - 2 * ch) * d
                take = ((d == 0) & has_right) | ((d == 1) & has_left)
            return remote(extb.at[k, pl.ds(at, ch)], extb.at[k, pl.ds(at, ch)],
                          fsem_s.at[k, which], fsem_r.at[k, which], t, other), take

        def start_halo(k, which):
            give = piece(k, which)[3]

            @pl.when(give)
            def _():
                halo(k, which).start()

        def finish_halo(k):
            for which in (0, 1, 2):
                take = piece(k, which)[4]

                @pl.when(take)
                def _():
                    halo(k, which).wait_recv()
                    forward(k, which).start()
            for which in (0, 1, 2):
                cp, take = forwarded(k, which)

                @pl.when(take)
                def _():
                    cp.wait_recv()

        def drain_halo(k):
            for which in (0, 1, 2):
                src, at, tile, give, take = piece(k, which)

                @pl.when(give)
                def _():
                    halo(k, which).wait_send()

                @pl.when(take)
                def _():
                    forward(k, which).wait_send()

        to_right = remote(data_ref.at[:, pl.ds(rows - half, half)], dx.at[:, pl.ds(0, half)],
                          dsem_s.at[0], dsem_r.at[0], right, v)
        to_left = remote(data_ref.at[:, pl.ds(0, half)], dx.at[:, pl.ds(half + rows, half)],
                         dsem_s.at[1], dsem_r.at[1], left, v)

        cp_est.wait()
        extb[0, pl.ds(wide, rows)] = em[...].astype(BF16)
        for which in (0, 1, 2):
            start_halo(0, which)

        @pl.when(has_right)
        def _():
            to_right.start()

        @pl.when(has_left)
        def _():
            to_left.start()

        @pl.when(t == 0)
        def _():
            for k in range(ITERS):
                extb[k, pl.ds(0, wide)] = jnp.zeros((wide, ny, nz), BF16)
            for i in range(views):
                dx[i, pl.ds(0, half)] = jnp.zeros((half, ny, nz), BF16)

        @pl.when(t == tiles - 1)
        def _():
            for k in range(ITERS):
                extb[k, pl.ds(ext - wide, wide)] = jnp.zeros((wide, ny, nz), BF16)
            for i in range(views):
                dx[i, pl.ds(half + rows, half)] = jnp.zeros((half, ny, nz), BF16)

        for i in range(views):
            zb[i, pl.ds(ext * ST, (ext_pad - ext) * ST), :] = jnp.zeros(((ext_pad - ext) * ST, nz), F32)
            rb[i, pl.ds(mid * ST, (mid_pad - mid) * ST), :] = jnp.zeros(((mid_pad - mid) * ST, nz), F32)

        def blur_z(k):
            step = ext // 10

            def body(j, _):
                lhs = extb[k, pl.ds(j * step, step)].reshape(step * ny, nz)
                o = dot(jnp.concatenate([lhs, lhs], axis=1), zf[...])
                for q in range(step):
                    for i in range(views):
                        zb[i, pl.ds((j * step + q) * ST, ny), :] = o[q * ny:(q + 1) * ny, i * nz:(i + 1) * nz]
                return 0
            lax.fori_loop(0, 10, body, 0)

        def conv_x(src, dst, w, n_in, n_out):
            def body(j, _):
                outs = []
                for u in range(GROUP):
                    y = 2 * (GROUP * j + u)
                    for i in range(views):
                        a = src[i, pl.ds(y, n_in, stride=ST), :]
                        b = src[i, pl.ds(y + 1, n_in, stride=ST), :]
                        r = jnp.concatenate([a, b], axis=1).astype(BF16)
                        outs.append((y, i, dot(w[i], jnp.concatenate([r, r], axis=0))))
                for y, i, o in outs:
                    dst[i, pl.ds(y, n_out, stride=ST), :] = o[:, :nz]
                    dst[i, pl.ds(y + 1, n_out, stride=ST), :] = o[:, nz:]
                return 0
            lax.fori_loop(0, ny // (2 * GROUP), body, 0)

        def ratios():
            def body(j, _):
                outs = []
                for u in range(5):
                    at = (5 * j + u) * 2 * ST
                    for i in range(views):
                        r = jnp.concatenate([xb[i, pl.ds(at, ny), :], xb[i, pl.ds(at + ST, ny), :]], axis=1).astype(BF16)
                        o = dot(yf[i], jnp.concatenate([r, r], axis=0))
                        row = 2 * (5 * j + u)
                        outs.append((at, i, dx[i, row].astype(F32) / o[:, :nz],
                                     dx[i, row + 1].astype(F32) / o[:, nz:]))
                for at, i, p, q in outs:
                    rb[i, pl.ds(at, ny), :] = p
                    rb[i, pl.ds(at + ST, ny), :] = q
                return 0
            lax.fori_loop(0, mid // 10, body, 0)

        def adjoint_rows(row):
            for j in range(ch // 2):
                at = (row + 2 * j) * ST
                to = j * 2 * ny
                for i in range(views):
                    r = jnp.concatenate([ab[i, pl.ds(at, ny), :], ab[i, pl.ds(at + ST, ny), :]], axis=1)
                    hi, lo = split(r)
                    o = dot(ya[i], jnp.concatenate([hi, hi, lo], axis=0))
                    yb[pl.ds(to, ny), i * nz:(i + 1) * nz] = o[:, :nz]
                    yb[pl.ds(to + ny, ny), i * nz:(i + 1) * nz] = o[:, nz:]
            hi, lo = split(yb[...])
            o = dot(hi, za[...])
            o = o[:, :nz] + o[:, nz:] + dot(lo, za[:, :nz])
            return o.reshape(ch, ny, nz)

        def partner(k, p):
            return remote(ps.at[k, p], pr.at[k, p], psem_s.at[k, p], psem_r.at[k, p], t, other)

        def over(k, p):
            return remote(hs.at[k, p], hr.at[k, p], ysem_s.at[k, p], ysem_r.at[k, p], t, across)

        def share(k, p):
            row = (inner, outer)[p]
            return remote(own(k + 1, row), own(k + 1, row), osem_s.at[k, p], osem_r.at[k, p], t, other)

        def shared(k, p):
            row = (ch + ch * (1 - c), 3 * ch * (1 - c))[p]
            return remote(own(k + 1, row), own(k + 1, row), osem_s.at[k, p], osem_r.at[k, p], t, other)

        finish_halo(0)
        cp_dat.wait()

        def iteration(k, _):
            blur_z(k)
            conv_x(zb, xb, xf, ext_pad, mid_pad)

            @pl.when((k == 0) & has_left)
            def _():
                to_right.wait_recv()

            @pl.when((k == 0) & has_right)
            def _():
                to_left.wait_recv()

            ratios()
            conv_x(rb, ab, xa, mid_pad, rows)
            theirs = (ch + ch * (1 - c), 3 * ch * (1 - c))
            ours = (inner, outer)
            for p in (0, 1):
                ps[k, p] = adjoint_rows(theirs[p])
                partner(k, p).start()
                po[p] = adjoint_rows(ours[p])
                partner(k, p).wait_recv()
                hs[k, p] = po[p] + pr[k, p]
                over(k, p).start()
            for p in (0, 1):
                over(k, p).wait_recv()
                rows_here = pl.ds(ours[p], ch)
                em[rows_here] = em[rows_here] * (hs[k, p] + hr[k, p]) / total_views

                @pl.when(k < ITERS - 1)
                def _():
                    extb[k + 1, pl.ds(wide + ours[p], ch)] = em[rows_here].astype(BF16)
                    for which in ((0, 1), (2,))[p]:
                        start_halo(k + 1, which)
                    share(k, p).start()

            @pl.when(k < ITERS - 1)
            def _():
                finish_halo(k + 1)
                for p in (0, 1):
                    shared(k, p).wait_recv()
            return 0

        lax.fori_loop(0, ITERS, iteration, 0)

        ends = []
        for p in (0, 1):
            row = (inner, outer)[p]
            fin[p] = em[pl.ds(row, ch)]
            here = pltpu.make_async_copy(fin.at[p], out_ref.at[pl.ds(row, ch)], lsem.at[2 + p])
            there = remote(fin.at[p], out_ref.at[pl.ds(row, ch)],
                           osem_s.at[ITERS - 1, p], osem_r.at[ITERS - 1, p], t, other)
            here.start()
            there.start()
            ends += [here, there]
        for cp in ends:
            cp.wait()

        @pl.when(has_right)
        def _():
            to_right.wait_send()

        @pl.when(has_left)
        def _():
            to_left.wait_send()

        for k in range(ITERS):
            drain_halo(k)
            for p in (0, 1):
                partner(k, p).wait_send()
                over(k, p).wait_send()
                if k < ITERS - 1:
                    share(k, p).wait_send()

    vmem = pltpu.VMEM
    dma = pltpu.SemaphoreType.DMA
    block = (ch, ny, nz)
    return pl.pallas_call(
        kernel,
        out_shape=jax.ShapeDtypeStruct(estimate.shape, F32),
        in_specs=[pl.BlockSpec(memory_space=pl.ANY)] * 2 + [pl.BlockSpec(memory_space=vmem)] * 6,
        out_specs=pl.BlockSpec(memory_space=pl.ANY),
        scratch_shapes=[
            vmem((ITERS, ext, ny, nz), BF16),
            vmem((views, ext_pad * ST, nz), F32),
            vmem((views, mid_pad * ST, nz), F32),
            vmem((views, mid_pad * ST, nz), F32),
            vmem((views, rows * ST, nz), F32),
            vmem((ch * ny, views * nz), F32),
            vmem((views, mid, ny, nz), BF16),
            vmem((rows, ny, nz), F32),
            vmem((ITERS, 2) + block, F32),
            vmem((ITERS, 2) + block, F32),
            vmem((2,) + block, F32),
            vmem((ITERS, 2) + block, F32),
            vmem((ITERS, 2) + block, F32),
            vmem((2,) + block, F32),
            dma((4,)), dma((2,)), dma((2,)),
            dma((ITERS, 3)), dma((ITERS, 3)), dma((ITERS, 3)), dma((ITERS, 3)),
            dma((ITERS, 2)), dma((ITERS, 2)), dma((ITERS, 2)), dma((ITERS, 2)),
            dma((ITERS, 2)), dma((ITERS, 2)),
        ],
        compiler_params=pltpu.CompilerParams(
            collective_id=0, has_side_effects=True, vmem_limit_bytes=60 * 1024 * 1024),
    )(data, estimate, *weights)


def solution(mesh):
    placed = (P("view", "tile", None, None), P("tile", None, None), P("view", None, None))
    return jax.shard_map(
        shards, mesh=mesh, in_specs=placed, out_specs=P("tile", None, None), check_vma=False
    )
```

```python
import jax
import jax.numpy as jnp
from jax import lax
from jax.experimental import pallas as pl
from jax.experimental.pallas import tpu as pltpu
from jax.sharding import PartitionSpec as P

ITERS = 3
TAPS = 31
GROUP = 4
ST = 65
F32 = jnp.float32
BF16 = jnp.bfloat16
MESH = pl.DeviceIdType.MESH


def split(w):
    hi = w.astype(BF16)
    return hi, (w - hi.astype(F32)).astype(BF16)


def dot(a, b):
    return jnp.dot(a, b, preferred_element_type=F32)


def band(tap, n_rows, n_cols, blocks, shift, low):
    col = lax.broadcasted_iota(jnp.int32, (n_rows, blocks * n_cols), 1)
    row = lax.broadcasted_iota(jnp.int32, (n_rows, blocks * n_cols), 0)
    is_low = jnp.zeros(col.shape, jnp.bool_)
    at = col
    for i in range(1, blocks):
        at = jnp.where(col >= i * n_cols, col - i * n_cols, at)
    for i in low:
        is_low = (col >= i * n_cols) & (col < (i + 1) * n_cols)
    offset = at - row + shift
    w = jnp.zeros(col.shape, F32)
    for k in range(TAPS):
        w = jnp.where(offset == k, tap(k), w)
    hi = w.astype(BF16).astype(F32)
    return jnp.where(is_low, w - hi, hi).astype(BF16)


def shards(data, estimate, psf_taps):
    views, rows, ny, nz = data.shape
    half = psf_taps.shape[2] // 2
    total_views = views * lax.axis_size("view")
    tiles = lax.axis_size("tile")
    wide = 2 * half
    ext = rows + 2 * wide
    mid = rows + 2 * half
    ext_pad = -(-ext // 16) * 16
    mid_pad = -(-mid // 16) * 16
    ch = rows // 4

    def kernel(data_ref, est_ref, taps, out_ref, xf, yf, zf, xa, ya, za,
               extb, zb, xb, rb, ab, yb, dx, em, ps, pr, po, hs, hr, fin,
               lsem, dsem_s, dsem_r, hsem_s, hsem_r, fsem_s, fsem_r,
               psem_s, psem_r, ysem_s, ysem_r, osem_s, osem_r):
        t = lax.axis_index("tile")
        v = lax.axis_index("view")
        c = lax.rem(v, 2)
        other = (v - c) + (1 - c)
        across = lax.rem(v + 2, 4)
        left = lax.rem(t + tiles - 1, tiles)
        right = lax.rem(t + 1, tiles)
        has_left = t > 0
        has_right = t < tiles - 1

        cp_est = pltpu.make_async_copy(est_ref, em, lsem.at[0])
        cp_dat = pltpu.make_async_copy(data_ref, dx.at[:, pl.ds(half, rows)], lsem.at[1])
        cp_est.start()
        cp_dat.start()

        barrier = pltpu.get_barrier_semaphore()
        for who in ((t, other), (t, across), (left, v), (right, v)):
            pl.semaphore_signal(barrier, inc=1, device_id=(who[1], who[0]), device_id_type=MESH)
        pl.semaphore_wait(barrier, 4)

        def remote(src, dst, s_sem, r_sem, tile, view):
            return pltpu.make_async_remote_copy(
                src_ref=src, dst_ref=dst, send_sem=s_sem, recv_sem=r_sem,
                device_id=(view, tile), device_id_type=MESH)

        inner = ch + ch * c
        outer = 3 * ch * c
        c_tile = jnp.where(c == 0, left, right)
        c_send = ((c == 0) & has_left) | ((c == 1) & has_right)
        c_recv = ((c == 0) & has_right) | ((c == 1) & has_left)

        def own(k, row):
            return extb.at[k, pl.ds(wide + row, ch)]

        def piece(k, which):
            if which == 0:
                src, at, tile, give, take = inner, ext - wide + ch + ch * c, left, has_left, has_right
            elif which == 1:
                src, at, tile, give, take = inner, ch * c, right, has_right, has_left
            else:
                src, at, tile, give, take = outer, (ext - wide) - (ext - wide - 2 * ch) * c, c_tile, c_send, c_recv
            return src, at, tile, give, take

        def halo(k, which):
            src, at, tile, give, take = piece(k, which)
            return remote(own(k, src), extb.at[k, pl.ds(at, ch)],
                          hsem_s.at[k, which], hsem_r.at[k, which], tile, v)

        def forward(k, which):
            src, at, tile, give, take = piece(k, which)
            return remote(extb.at[k, pl.ds(at, ch)], extb.at[k, pl.ds(at, ch)],
                          fsem_s.at[k, which], fsem_r.at[k, which], t, other)

        def forwarded(k, which):
            d = 1 - c
            if which == 0:
                at, take = ext - wide + ch + ch * d, has_right
            elif which == 1:
                at, take = ch * d, has_left
            else:
                at = (ext - wide) - (ext - wide - 2 * ch) * d
                take = ((d == 0) & has_right) | ((d == 1) & has_left)
            return remote(extb.at[k, pl.ds(at, ch)], extb.at[k, pl.ds(at, ch)],
                          fsem_s.at[k, which], fsem_r.at[k, which], t, other), at, take

        def start_halo(k, which):
            give = piece(k, which)[3]

            @pl.when(give)
            def _():
                halo(k, which).start()

        def finish_halo(k, between):
            def arrive(which):
                at, take = piece(k, which)[1], piece(k, which)[4]

                @pl.when(take)
                def _():
                    halo(k, which).wait_recv()
                    forward(k, which).start()

            arrive(0)
            arrive(1)
            between()
            blur_z(k, piece(k, 0)[1])
            blur_z(k, piece(k, 1)[1])
            arrive(2)
            blur_z(k, piece(k, 2)[1])
            for which in (0, 1, 2):
                cp, at, take = forwarded(k, which)

                @pl.when(take)
                def _():
                    cp.wait_recv()
                blur_z(k, at)

        def drain_halo(k):
            for which in (0, 1, 2):
                src, at, tile, give, take = piece(k, which)

                @pl.when(give)
                def _():
                    halo(k, which).wait_send()

                @pl.when(take)
                def _():
                    forward(k, which).wait_send()

        to_right = remote(data_ref.at[:, pl.ds(rows - half, half)], dx.at[:, pl.ds(0, half)],
                          dsem_s.at[0], dsem_r.at[0], right, v)
        to_left = remote(data_ref.at[:, pl.ds(0, half)], dx.at[:, pl.ds(half + rows, half)],
                         dsem_s.at[1], dsem_r.at[1], left, v)

        cp_est.wait()
        extb[0, pl.ds(wide, rows)] = em[...].astype(BF16)
        for which in (0, 1, 2):
            start_halo(0, which)

        @pl.when(has_right)
        def _():
            to_right.start()

        @pl.when(has_left)
        def _():
            to_left.start()

        @pl.when(t == 0)
        def _():
            for k in range(ITERS):
                extb[k, pl.ds(0, wide)] = jnp.zeros((wide, ny, nz), BF16)
            for i in range(views):
                dx[i, pl.ds(0, half)] = jnp.zeros((half, ny, nz), BF16)

        @pl.when(t == tiles - 1)
        def _():
            for k in range(ITERS):
                extb[k, pl.ds(ext - wide, wide)] = jnp.zeros((wide, ny, nz), BF16)
            for i in range(views):
                dx[i, pl.ds(half + rows, half)] = jnp.zeros((half, ny, nz), BF16)

        for i in range(views):
            zb[i, pl.ds(ext * ST, (ext_pad - ext) * ST), :] = jnp.zeros(((ext_pad - ext) * ST, nz), F32)
            rb[i, pl.ds(mid * ST, (mid_pad - mid) * ST), :] = jnp.zeros(((mid_pad - mid) * ST, nz), F32)

        for i in range(views):
            def forth(d, i=i):
                return lambda q: taps[i, d, q]

            def back(d, i=i):
                return lambda q: taps[i, d, TAPS - 1 - q]

            w = band(back(2), nz, nz, 2, half, (1,))
            zf[pl.ds(0, nz), i * nz:(i + 1) * nz] = w[:, :nz]
            zf[pl.ds(nz, nz), i * nz:(i + 1) * nz] = w[:, nz:]
            xf[i] = band(forth(0), mid_pad, ext_pad, 2, 0, (1,))
            yf[i] = band(forth(1), ny, ny, 2, half, (1,))
            xa[i] = band(back(0), rows, mid_pad, 2, 0, (1,))
            ya[i] = band(back(1), ny, ny, 3, half, (1,))
            za[pl.ds(i * nz, nz), :] = band(forth(2), nz, nz, 2, half, (1,))

        def blur_z(k, row):
            lhs = extb[k, pl.ds(row, ch)].reshape(ch * ny, nz)
            o = dot(jnp.concatenate([lhs, lhs], axis=1), zf[...])
            for q in range(ch):
                for i in range(views):
                    zb[i, pl.ds((row + q) * ST, ny), :] = o[q * ny:(q + 1) * ny, i * nz:(i + 1) * nz]

        def conv_x(src, dst, w, n_in, n_out):
            def body(j, _):
                outs = []
                for u in range(GROUP):
                    y = 2 * (GROUP * j + u)
                    for i in range(views):
                        a = src[i, pl.ds(y, n_in, stride=ST), :]
                        b = src[i, pl.ds(y + 1, n_in, stride=ST), :]
                        r = jnp.concatenate([a, b], axis=1).astype(BF16)
                        outs.append((y, i, dot(w[i], jnp.concatenate([r, r], axis=0))))
                for y, i, o in outs:
                    dst[i, pl.ds(y, n_out, stride=ST), :] = o[:, :nz]
                    dst[i, pl.ds(y + 1, n_out, stride=ST), :] = o[:, nz:]
                return 0
            lax.fori_loop(0, ny // (2 * GROUP), body, 0)

        def ratios():
            def body(j, _):
                outs = []
                for u in range(5):
                    at = (5 * j + u) * 2 * ST
                    for i in range(views):
                        r = jnp.concatenate([xb[i, pl.ds(at, ny), :], xb[i, pl.ds(at + ST, ny), :]], axis=1).astype(BF16)
                        o = dot(yf[i], jnp.concatenate([r, r], axis=0))
                        row = 2 * (5 * j + u)
                        outs.append((at, i, dx[i, row].astype(F32) / o[:, :nz],
                                     dx[i, row + 1].astype(F32) / o[:, nz:]))
                for at, i, p, q in outs:
                    rb[i, pl.ds(at, ny), :] = p
                    rb[i, pl.ds(at + ST, ny), :] = q
                return 0
            lax.fori_loop(0, mid // 10, body, 0)

        def adjoint_rows(row):
            for j in range(ch // 2):
                at = (row + 2 * j) * ST
                to = j * 2 * ny
                for i in range(views):
                    r = jnp.concatenate([ab[i, pl.ds(at, ny), :], ab[i, pl.ds(at + ST, ny), :]], axis=1)
                    hi, lo = split(r)
                    o = dot(ya[i], jnp.concatenate([hi, hi, lo], axis=0))
                    yb[pl.ds(to, ny), i * nz:(i + 1) * nz] = o[:, :nz]
                    yb[pl.ds(to + ny, ny), i * nz:(i + 1) * nz] = o[:, nz:]
            hi, lo = split(yb[...])
            o = dot(hi, za[...])
            o = o[:, :nz] + o[:, nz:] + dot(lo, za[:, :nz])
            return o.reshape(ch, ny, nz)

        def partner(k, p):
            return remote(ps.at[k, p], pr.at[k, p], psem_s.at[k, p], psem_r.at[k, p], t, other)

        def over(k, p):
            return remote(hs.at[k, p], hr.at[k, p], ysem_s.at[k, p], ysem_r.at[k, p], t, across)

        def share(k, p):
            row = (inner, outer)[p]
            return remote(own(k + 1, row), own(k + 1, row), osem_s.at[k, p], osem_r.at[k, p], t, other)

        def shared(k, p):
            row = (ch + ch * (1 - c), 3 * ch * (1 - c))[p]
            return remote(own(k + 1, row), own(k + 1, row), osem_s.at[k, p], osem_r.at[k, p], t, other)

        for p in range(4):
            blur_z(0, wide + ch * p)
        finish_halo(0, lambda: None)
        cp_dat.wait()

        def iteration(k, _):
            conv_x(zb, xb, xf, ext_pad, mid_pad)

            @pl.when((k == 0) & has_left)
            def _():
                to_right.wait_recv()

            @pl.when((k == 0) & has_right)
            def _():
                to_left.wait_recv()

            ratios()
            conv_x(rb, ab, xa, mid_pad, rows)
            theirs = (ch + ch * (1 - c), 3 * ch * (1 - c))
            ours = (inner, outer)
            for p in (0, 1):
                ps[k, p] = adjoint_rows(theirs[p])
                partner(k, p).start()
                po[p] = adjoint_rows(ours[p])
                partner(k, p).wait_recv()
                hs[k, p] = po[p] + pr[k, p]
                over(k, p).start()
            for p in (0, 1):
                over(k, p).wait_recv()
                rows_here = pl.ds(ours[p], ch)
                em[rows_here] = em[rows_here] * (hs[k, p] + hr[k, p]) / total_views

                @pl.when(k < ITERS - 1)
                def _():
                    extb[k + 1, pl.ds(wide + ours[p], ch)] = em[rows_here].astype(BF16)
                    for which in ((0, 1), (2,))[p]:
                        start_halo(k + 1, which)
                    share(k, p).start()
                    blur_z(k + 1, wide + ours[p])

            @pl.when(k < ITERS - 1)
            def _():
                def between():
                    for p in (0, 1):
                        shared(k, p).wait_recv()
                        blur_z(k + 1, wide + theirs[p])
                finish_halo(k + 1, between)
            return 0

        lax.fori_loop(0, ITERS, iteration, 0)

        ends = []
        for p in (0, 1):
            row = (inner, outer)[p]
            fin[p] = em[pl.ds(row, ch)]
            here = pltpu.make_async_copy(fin.at[p], out_ref.at[pl.ds(row, ch)], lsem.at[2 + p])
            there = remote(fin.at[p], out_ref.at[pl.ds(row, ch)],
                           osem_s.at[ITERS - 1, p], osem_r.at[ITERS - 1, p], t, other)
            here.start()
            there.start()
            ends += [here, there]
        for cp in ends:
            cp.wait()

        @pl.when(has_right)
        def _():
            to_right.wait_send()

        @pl.when(has_left)
        def _():
            to_left.wait_send()

        for k in range(ITERS):
            drain_halo(k)
            for p in (0, 1):
                partner(k, p).wait_send()
                over(k, p).wait_send()
                if k < ITERS - 1:
                    share(k, p).wait_send()

    vmem = pltpu.VMEM
    dma = pltpu.SemaphoreType.DMA
    block = (ch, ny, nz)
    return pl.pallas_call(
        kernel,
        out_shape=jax.ShapeDtypeStruct(estimate.shape, F32),
        in_specs=[pl.BlockSpec(memory_space=pl.ANY)] * 2 + [pl.BlockSpec(memory_space=pltpu.SMEM)],
        out_specs=pl.BlockSpec(memory_space=pl.ANY),
        scratch_shapes=[
            vmem((views, mid_pad, 2 * ext_pad), BF16),
            vmem((views, ny, 2 * ny), BF16),
            vmem((2 * nz, 2 * nz), BF16),
            vmem((views, rows, 2 * mid_pad), BF16),
            vmem((views, ny, 3 * ny), BF16),
            vmem((2 * nz, 2 * nz), BF16),
            vmem((ITERS, ext, ny, nz), BF16),
            vmem((views, ext_pad * ST, nz), F32),
            vmem((views, mid_pad * ST, nz), F32),
            vmem((views, mid_pad * ST, nz), F32),
            vmem((views, rows * ST, nz), F32),
            vmem((ch * ny, views * nz), F32),
            vmem((views, mid, ny, nz), BF16),
            vmem((rows, ny, nz), F32),
            vmem((ITERS, 2) + block, F32),
            vmem((ITERS, 2) + block, F32),
            vmem((2,) + block, F32),
            vmem((ITERS, 2) + block, F32),
            vmem((ITERS, 2) + block, F32),
            vmem((2,) + block, F32),
            dma((4,)), dma((2,)), dma((2,)),
            dma((ITERS, 3)), dma((ITERS, 3)), dma((ITERS, 3)), dma((ITERS, 3)),
            dma((ITERS, 2)), dma((ITERS, 2)), dma((ITERS, 2)), dma((ITERS, 2)),
            dma((ITERS, 2)), dma((ITERS, 2)),
        ],
        compiler_params=pltpu.CompilerParams(
            collective_id=0, has_side_effects=True, vmem_limit_bytes=60 * 1024 * 1024),
    )(data, estimate, psf_taps)


def solution(mesh):
    placed = (P("view", "tile", None, None), P("tile", None, None), P("view", None, None))
    return jax.shard_map(
        shards, mesh=mesh, in_specs=placed, out_specs=P("tile", None, None), check_vma=False
    )
```

```python
import jax
import jax.numpy as jnp
from jax import lax
from jax.experimental import pallas as pl
from jax.experimental.pallas import tpu as pltpu
from jax.sharding import PartitionSpec as P

ITERS = 3
TAPS = 31
GROUP = 4
ST = 65
F32 = jnp.float32
BF16 = jnp.bfloat16
MESH = pl.DeviceIdType.MESH


def split(w):
    hi = w.astype(BF16)
    return hi, (w - hi.astype(F32)).astype(BF16)


TOP = 2.0 ** 7.5


def encode(h, m):
    w = jnp.maximum(h * (TOP / m), 1.0 / TOP)
    for _ in range(4):
        w = w * w
    return w.astype(BF16)


def decode(code, m):
    return jnp.exp(jnp.log(code.astype(F32)) * 0.0625) * (m * (1.0 / TOP))


def dot(a, b):
    return jnp.dot(a, b, preferred_element_type=F32)


def band(tap, n_rows, n_cols, blocks, shift, low):
    col = lax.broadcasted_iota(jnp.int32, (n_rows, blocks * n_cols), 1)
    row = lax.broadcasted_iota(jnp.int32, (n_rows, blocks * n_cols), 0)
    is_low = jnp.zeros(col.shape, jnp.bool_)
    at = col
    for i in range(1, blocks):
        at = jnp.where(col >= i * n_cols, col - i * n_cols, at)
    for i in low:
        is_low = (col >= i * n_cols) & (col < (i + 1) * n_cols)
    offset = at - row + shift
    w = jnp.zeros(col.shape, F32)
    for k in range(TAPS):
        w = jnp.where(offset == k, tap(k), w)
    hi = w.astype(BF16).astype(F32)
    return jnp.where(is_low, w - hi, hi).astype(BF16)


def shards(data, estimate, psf_taps):
    views, rows, ny, nz = data.shape
    half = psf_taps.shape[2] // 2
    total_views = views * lax.axis_size("view")
    tiles = lax.axis_size("tile")
    wide = 2 * half
    ext = rows + 2 * wide
    mid = rows + 2 * half
    ext_pad = -(-ext // 16) * 16
    mid_pad = -(-mid // 16) * 16
    ch = rows // 4

    def kernel(data_ref, est_ref, taps, out_ref, xf, yf, zf, xa, ya, za,
               extb, zb, xb, rb, ab, yb, dx, em, ps, pr, po, hs, hr, ms, mr, fin,
               lsem, dsem_s, dsem_r, hsem_s, hsem_r, fsem_s, fsem_r,
               psem_s, psem_r, ysem_s, ysem_r, osem_s, osem_r, msem_s, msem_r):
        t = lax.axis_index("tile")
        v = lax.axis_index("view")
        c = lax.rem(v, 2)
        other = (v - c) + (1 - c)
        across = lax.rem(v + 2, 4)
        left = lax.rem(t + tiles - 1, tiles)
        right = lax.rem(t + 1, tiles)
        has_left = t > 0
        has_right = t < tiles - 1

        cp_est = pltpu.make_async_copy(est_ref, em, lsem.at[0])
        cp_dat = pltpu.make_async_copy(data_ref, dx.at[:, pl.ds(half, rows)], lsem.at[1])
        cp_est.start()
        cp_dat.start()

        barrier = pltpu.get_barrier_semaphore()
        for who in ((t, other), (t, across), (left, v), (right, v)):
            pl.semaphore_signal(barrier, inc=1, device_id=(who[1], who[0]), device_id_type=MESH)
        pl.semaphore_wait(barrier, 4)

        def remote(src, dst, s_sem, r_sem, tile, view):
            return pltpu.make_async_remote_copy(
                src_ref=src, dst_ref=dst, send_sem=s_sem, recv_sem=r_sem,
                device_id=(view, tile), device_id_type=MESH)

        inner = ch + ch * c
        outer = 3 * ch * c
        c_tile = jnp.where(c == 0, left, right)
        c_send = ((c == 0) & has_left) | ((c == 1) & has_right)
        c_recv = ((c == 0) & has_right) | ((c == 1) & has_left)

        def own(k, row):
            return extb.at[k, pl.ds(wide + row, ch)]

        def piece(k, which):
            if which == 0:
                src, at, tile, give, take = inner, ext - wide + ch + ch * c, left, has_left, has_right
            elif which == 1:
                src, at, tile, give, take = inner, ch * c, right, has_right, has_left
            else:
                src, at, tile, give, take = outer, (ext - wide) - (ext - wide - 2 * ch) * c, c_tile, c_send, c_recv
            return src, at, tile, give, take

        def halo(k, which):
            src, at, tile, give, take = piece(k, which)
            return remote(own(k, src), extb.at[k, pl.ds(at, ch)],
                          hsem_s.at[k, which], hsem_r.at[k, which], tile, v)

        def forward(k, which):
            src, at, tile, give, take = piece(k, which)
            return remote(extb.at[k, pl.ds(at, ch)], extb.at[k, pl.ds(at, ch)],
                          fsem_s.at[k, which], fsem_r.at[k, which], t, other)

        def forwarded(k, which):
            d = 1 - c
            if which == 0:
                at, take = ext - wide + ch + ch * d, has_right
            elif which == 1:
                at, take = ch * d, has_left
            else:
                at = (ext - wide) - (ext - wide - 2 * ch) * d
                take = ((d == 0) & has_right) | ((d == 1) & has_left)
            return remote(extb.at[k, pl.ds(at, ch)], extb.at[k, pl.ds(at, ch)],
                          fsem_s.at[k, which], fsem_r.at[k, which], t, other), at, take

        def start_halo(k, which):
            give = piece(k, which)[3]

            @pl.when(give)
            def _():
                halo(k, which).start()

        def finish_halo(k, between):
            def arrive(which):
                at, take = piece(k, which)[1], piece(k, which)[4]

                @pl.when(take)
                def _():
                    halo(k, which).wait_recv()
                    forward(k, which).start()

            arrive(0)
            arrive(1)
            between()
            blur_z(k, piece(k, 0)[1])
            blur_z(k, piece(k, 1)[1])
            arrive(2)
            blur_z(k, piece(k, 2)[1])
            for which in (0, 1, 2):
                cp, at, take = forwarded(k, which)

                @pl.when(take)
                def _():
                    cp.wait_recv()
                blur_z(k, at)

        def drain_halo(k):
            for which in (0, 1, 2):
                src, at, tile, give, take = piece(k, which)

                @pl.when(give)
                def _():
                    halo(k, which).wait_send()

                @pl.when(take)
                def _():
                    forward(k, which).wait_send()

        to_right = remote(data_ref.at[:, pl.ds(rows - half, half)], dx.at[:, pl.ds(0, half)],
                          dsem_s.at[0], dsem_r.at[0], right, v)
        to_left = remote(data_ref.at[:, pl.ds(0, half)], dx.at[:, pl.ds(half + rows, half)],
                         dsem_s.at[1], dsem_r.at[1], left, v)

        cp_est.wait()
        extb[0, pl.ds(wide, rows)] = em[...].astype(BF16)
        for which in (0, 1, 2):
            start_halo(0, which)

        @pl.when(has_right)
        def _():
            to_right.start()

        @pl.when(has_left)
        def _():
            to_left.start()

        @pl.when(t == 0)
        def _():
            for k in range(ITERS):
                extb[k, pl.ds(0, wide)] = jnp.zeros((wide, ny, nz), BF16)
            for i in range(views):
                dx[i, pl.ds(0, half)] = jnp.zeros((half, ny, nz), BF16)

        @pl.when(t == tiles - 1)
        def _():
            for k in range(ITERS):
                extb[k, pl.ds(ext - wide, wide)] = jnp.zeros((wide, ny, nz), BF16)
            for i in range(views):
                dx[i, pl.ds(half + rows, half)] = jnp.zeros((half, ny, nz), BF16)

        for i in range(views):
            zb[i, pl.ds(ext * ST, (ext_pad - ext) * ST), :] = jnp.zeros(((ext_pad - ext) * ST, nz), F32)
            rb[i, pl.ds(mid * ST, (mid_pad - mid) * ST), :] = jnp.zeros(((mid_pad - mid) * ST, nz), F32)

        for i in range(views):
            def forth(d, i=i):
                return lambda q: taps[i, d, q]

            def back(d, i=i):
                return lambda q: taps[i, d, TAPS - 1 - q]

            w = band(back(2), nz, nz, 2, half, (1,))
            zf[pl.ds(0, nz), i * nz:(i + 1) * nz] = w[:, :nz]
            zf[pl.ds(nz, nz), i * nz:(i + 1) * nz] = w[:, nz:]
            xf[i] = band(forth(0), mid_pad, ext_pad, 2, 0, (1,))
            yf[i] = band(forth(1), ny, ny, 2, half, (1,))
            xa[i] = band(back(0), rows, mid_pad, 2, 0, (1,))
            ya[i] = band(back(1), ny, ny, 3, half, (1,))
            za[pl.ds(i * nz, nz), :] = band(forth(2), nz, nz, 2, half, (1,))

        def blur_z(k, row):
            lhs = extb[k, pl.ds(row, ch)].reshape(ch * ny, nz)
            o = dot(jnp.concatenate([lhs, lhs], axis=1), zf[...])
            for q in range(ch):
                for i in range(views):
                    zb[i, pl.ds((row + q) * ST, ny), :] = o[q * ny:(q + 1) * ny, i * nz:(i + 1) * nz]

        def conv_x(src, dst, w, n_in, n_out):
            def body(j, _):
                outs = []
                for u in range(GROUP):
                    y = 2 * (GROUP * j + u)
                    for i in range(views):
                        a = src[i, pl.ds(y, n_in, stride=ST), :]
                        b = src[i, pl.ds(y + 1, n_in, stride=ST), :]
                        r = jnp.concatenate([a, b], axis=1).astype(BF16)
                        outs.append((y, i, dot(w[i], jnp.concatenate([r, r], axis=0))))
                for y, i, o in outs:
                    dst[i, pl.ds(y, n_out, stride=ST), :] = o[:, :nz]
                    dst[i, pl.ds(y + 1, n_out, stride=ST), :] = o[:, nz:]
                return 0
            lax.fori_loop(0, ny // (2 * GROUP), body, 0)

        def ratios():
            def body(j, _):
                outs = []
                for u in range(5):
                    at = (5 * j + u) * 2 * ST
                    for i in range(views):
                        r = jnp.concatenate([xb[i, pl.ds(at, ny), :], xb[i, pl.ds(at + ST, ny), :]], axis=1).astype(BF16)
                        o = dot(yf[i], jnp.concatenate([r, r], axis=0))
                        row = 2 * (5 * j + u)
                        outs.append((at, i, dx[i, row].astype(F32) / o[:, :nz],
                                     dx[i, row + 1].astype(F32) / o[:, nz:]))
                for at, i, p, q in outs:
                    rb[i, pl.ds(at, ny), :] = p
                    rb[i, pl.ds(at + ST, ny), :] = q
                return 0
            lax.fori_loop(0, mid // 10, body, 0)

        def adjoint_rows(row):
            for j in range(ch // 2):
                at = (row + 2 * j) * ST
                to = j * 2 * ny
                for i in range(views):
                    r = jnp.concatenate([ab[i, pl.ds(at, ny), :], ab[i, pl.ds(at + ST, ny), :]], axis=1)
                    hi, lo = split(r)
                    o = dot(ya[i], jnp.concatenate([hi, hi, lo], axis=0))
                    yb[pl.ds(to, ny), i * nz:(i + 1) * nz] = o[:, :nz]
                    yb[pl.ds(to + ny, ny), i * nz:(i + 1) * nz] = o[:, nz:]
            hi, lo = split(yb[...])
            o = dot(hi, za[...])
            o = o[:, :nz] + o[:, nz:] + dot(lo, za[:, :nz])
            return o.reshape(ch, ny, nz)

        def partner(k, p):
            return remote(ps.at[k, p], pr.at[k, p], psem_s.at[k, p], psem_r.at[k, p], t, other)

        def over(k, p):
            return remote(hs.at[k, p], hr.at[k, p], ysem_s.at[k, p], ysem_r.at[k, p], t, across)

        def over_scale(k, p):
            return remote(ms.at[k, p], mr.at[k, p], msem_s.at[k, p], msem_r.at[k, p], t, across)

        def scale_of(ref, k, p):
            return ref[k, p].astype(F32)[:1].reshape(1, 1, nz)

        def share(k, p):
            row = (inner, outer)[p]
            return remote(own(k + 1, row), own(k + 1, row), osem_s.at[k, p], osem_r.at[k, p], t, other)

        def shared(k, p):
            row = (ch + ch * (1 - c), 3 * ch * (1 - c))[p]
            return remote(own(k + 1, row), own(k + 1, row), osem_s.at[k, p], osem_r.at[k, p], t, other)

        for p in range(4):
            blur_z(0, wide + ch * p)
        finish_halo(0, lambda: None)
        cp_dat.wait()

        def iteration(k, _):
            conv_x(zb, xb, xf, ext_pad, mid_pad)

            @pl.when((k == 0) & has_left)
            def _():
                to_right.wait_recv()

            @pl.when((k == 0) & has_right)
            def _():
                to_left.wait_recv()

            ratios()
            conv_x(rb, ab, xa, mid_pad, rows)
            theirs = (ch + ch * (1 - c), 3 * ch * (1 - c))
            ours = (inner, outer)
            for p in (0, 1):
                ps[k, p] = adjoint_rows(theirs[p])
                partner(k, p).start()
                po[p] = adjoint_rows(ours[p])
                partner(k, p).wait_recv()
                both = po[p] + pr[k, p]
                ms[k, p] = jnp.full((16, nz), jnp.max(both) * 1.01, F32).astype(BF16)
                hs[k, p] = encode(both, scale_of(ms, k, p))
                over_scale(k, p).start()
                over(k, p).start()
            for p in (0, 1):
                over_scale(k, p).wait_recv()
                over(k, p).wait_recv()
                total = decode(hs[k, p], scale_of(ms, k, p)) + decode(hr[k, p], scale_of(mr, k, p))
                rows_here = pl.ds(ours[p], ch)
                em[rows_here] = em[rows_here] * total / total_views

                @pl.when(k < ITERS - 1)
                def _():
                    extb[k + 1, pl.ds(wide + ours[p], ch)] = em[rows_here].astype(BF16)
                    for which in ((0, 1), (2,))[p]:
                        start_halo(k + 1, which)
                    share(k, p).start()
                    blur_z(k + 1, wide + ours[p])

            @pl.when(k < ITERS - 1)
            def _():
                def between():
                    for p in (0, 1):
                        shared(k, p).wait_recv()
                        blur_z(k + 1, wide + theirs[p])
                finish_halo(k + 1, between)
            return 0

        lax.fori_loop(0, ITERS, iteration, 0)

        ends = []
        for p in (0, 1):
            row = (inner, outer)[p]
            fin[p] = em[pl.ds(row, ch)]
            here = pltpu.make_async_copy(fin.at[p], out_ref.at[pl.ds(row, ch)], lsem.at[2 + p])
            there = remote(fin.at[p], out_ref.at[pl.ds(row, ch)],
                           osem_s.at[ITERS - 1, p], osem_r.at[ITERS - 1, p], t, other)
            here.start()
            there.start()
            ends += [here, there]
        for cp in ends:
            cp.wait()

        @pl.when(has_right)
        def _():
            to_right.wait_send()

        @pl.when(has_left)
        def _():
            to_left.wait_send()

        for k in range(ITERS):
            drain_halo(k)
            for p in (0, 1):
                partner(k, p).wait_send()
                over(k, p).wait_send()
                over_scale(k, p).wait_send()
                if k < ITERS - 1:
                    share(k, p).wait_send()

    vmem = pltpu.VMEM
    dma = pltpu.SemaphoreType.DMA
    block = (ch, ny, nz)
    return pl.pallas_call(
        kernel,
        out_shape=jax.ShapeDtypeStruct(estimate.shape, F32),
        in_specs=[pl.BlockSpec(memory_space=pl.ANY)] * 2 + [pl.BlockSpec(memory_space=pltpu.SMEM)],
        out_specs=pl.BlockSpec(memory_space=pl.ANY),
        scratch_shapes=[
            vmem((views, mid_pad, 2 * ext_pad), BF16),
            vmem((views, ny, 2 * ny), BF16),
            vmem((2 * nz, 2 * nz), BF16),
            vmem((views, rows, 2 * mid_pad), BF16),
            vmem((views, ny, 3 * ny), BF16),
            vmem((2 * nz, 2 * nz), BF16),
            vmem((ITERS, ext, ny, nz), BF16),
            vmem((views, ext_pad * ST, nz), F32),
            vmem((views, mid_pad * ST, nz), F32),
            vmem((views, mid_pad * ST, nz), F32),
            vmem((views, rows * ST, nz), F32),
            vmem((ch * ny, views * nz), F32),
            vmem((views, mid, ny, nz), BF16),
            vmem((rows, ny, nz), F32),
            vmem((ITERS, 2) + block, F32),
            vmem((ITERS, 2) + block, F32),
            vmem((2,) + block, F32),
            vmem((ITERS, 2) + block, BF16),
            vmem((ITERS, 2) + block, BF16),
            vmem((ITERS, 2, 16, nz), BF16),
            vmem((ITERS, 2, 16, nz), BF16),
            vmem((2,) + block, F32),
            dma((4,)), dma((2,)), dma((2,)),
            dma((ITERS, 3)), dma((ITERS, 3)), dma((ITERS, 3)), dma((ITERS, 3)),
            dma((ITERS, 2)), dma((ITERS, 2)), dma((ITERS, 2)), dma((ITERS, 2)),
            dma((ITERS, 2)), dma((ITERS, 2)), dma((ITERS, 2)), dma((ITERS, 2)),
        ],
        compiler_params=pltpu.CompilerParams(
            collective_id=0, has_side_effects=True, vmem_limit_bytes=60 * 1024 * 1024),
    )(data, estimate, psf_taps)


def solution(mesh):
    placed = (P("view", "tile", None, None), P("tile", None, None), P("view", None, None))
    return jax.shard_map(
        shards, mesh=mesh, in_specs=placed, out_specs=P("tile", None, None), check_vma=False
    )
```
